32 devices in a mesh: seq: 4 (over y, x), exp: 8 (over z, core).
Axes of the slice: x: 2, y: 2, z: 4, core: 2. Of those that a mesh axis runs over, the one named last changes fastest.
Arguments:
- inputs: bfloat16 [4096, 4096], P(('seq', 'exp')), may hold values from -6 to 6
- queries: bfloat16 [4096, 4096], P(('seq', 'exp')), may hold values from -40 to 40
- keys: bfloat16 [4096, 4096], P(('seq', 'exp')), may hold values from -4 to 4
- values: bfloat16 [4096, 4096], P(('seq', 'exp')), may hold values from -6 to 6
- norm_gain: float32 [4096], replicated, may hold values from 0.25 to 1.75
- expert_ids: int32 [4096, 2], P(('seq', 'exp')), may hold values from 0 to 7, all different within a row; in each aligned block of 128 rows (0 to 127, 128 to 255, ...) at most 32 rows name the same one
- gate_weights: float32 [4096, 2], P(('seq', 'exp')), may hold values from 0.2 to 1
- pairs: int32 [16, 2], replicated, may hold values from 0 to 7, as said below
- w_gate: bfloat16 [8, 4096, 4096], P('exp', None, 'seq'), may hold values from -0.09375 to 0.09375
- w_up: bfloat16 [8, 4096, 4096], P('exp', None, 'seq'), may hold values from -0.09375 to 0.09375
- w_down: bfloat16 [8, 4096, 4096], P('exp', 'seq'), may hold values from -0.09375 to 0.09375
Outputs:
- output: bfloat16 [4096, 4096], P(('seq', 'exp'))
The draws below stay inside these ranges and needn't reach their ends.
Inputs may be any that keep to these rules, and one draw needn't show every extreme that they name: `pairs`: each row is (query block, key block) with the key block from the query block - 2 to the query block; rows are distinct; every block is paired with itself; some pair has distance 2. `expert_ids`: the 2 ids of a token differ; within the 128 rows of one device every expert is named exactly 32 times.
All inputs are finite; a program needn't handle non-finite values.
Results may differ from the reference program's by a relative error of at most 0.007.
Values may be sent and summed in bfloat16 or wider, within the bound.
A program may use at most 128 MiB of HBM per device.

```python
import math
import jax
import jax.numpy as jnp
import numpy as np
from jax import lax

D = 4096
HEADS = 32
HSZ = 128
HD = 4096
FF = 4096
FFSLICE = 1024
EXPERTS = 8
TOP = 2
TOK_DEV = 128
TOKENS = 4096
CAP = 32
BLK = 512
DIST = 2
NBLK = 8
NEXTRA = 8
N_SEQ = 4


def drawn_fields(key):
    base_key = jax.random.fold_in(key, 7)
    key_first = jax.random.fold_in(base_key, 0)
    key_fourth = jax.random.fold_in(base_key, 3)
    key_field = jax.random.normal(key_first, (TOKENS, HD), jnp.float32)
    query_field = jax.random.normal(key_fourth, (TOKENS, HD), jnp.float32)
    return (jnp.clip(query_field, -40.0, 40.0), jnp.clip(key_field, -4.0, 4.0))


def draw_queries(key, part):
    return drawn_fields(key)[0].astype(jnp.bfloat16)


def draw_keys(key, part):
    return drawn_fields(key)[1].astype(jnp.bfloat16)


def draw_pairs(key, part):
    candidates = DIST * NBLK
    cand_index = jnp.arange(candidates, dtype=jnp.int32)
    query_block = cand_index // DIST
    distance = cand_index % DIST + 1
    priority = jax.random.permutation(jax.random.fold_in(key, 11), candidates).astype(jnp.int32)
    priority = jnp.where(query_block >= distance, priority, -1)
    priority = jnp.where((query_block == NBLK - 1) & (distance == DIST), candidates, priority)
    ignored, chosen = lax.top_k(priority, NEXTRA)
    extra_pairs = jnp.stack([query_block[chosen], query_block[chosen] - distance[chosen]], 1)
    block_ids = jnp.arange(NBLK, dtype=jnp.int32)
    diagonal = jnp.stack([block_ids, block_ids], 1)
    return jnp.concatenate([diagonal, extra_pairs], 0).astype(jnp.int32)


def steps_of(own_key, dims, cuts, low, top_value):
    factor_of = 1.0
    for dim, blocks in cuts:
        steps = jax.random.uniform(jax.random.fold_in(jax.random.fold_in(own_key, 6), dim), (blocks,), jnp.float32, low / len(cuts), top_value / len(cuts))
        factor_of = factor_of * jnp.repeat(jnp.exp(steps), dims[dim] // blocks).reshape((-1,) + (1,) * (len(dims) - 1 - dim))
    return factor_of


def deal_out(own_key, own, number, rows, count, top, reach, skew):
    sequence = jax.random.permutation(own_key, count)
    packed, common = shares(count, rows * top, reach, skew, True), shares(count, rows * top, reach, skew, False)
    places = jnp.arange(count)

    def named(sizes, rotation):
        used = int((sizes > 0).sum())
        fixed = max(1, used // 4)
        moved = fixed + (places - fixed + rotation * (used - fixed)) % max(1, count - fixed)
        return jnp.zeros((count,), jnp.int32).at[sequence[jnp.where(places < fixed, places, moved)]].set(jnp.asarray(sizes, jnp.int32))

    sizes = jnp.where(number % 4 == 0, named(packed, number // 4), named(common, number - number // 4 - 1))
    mixed = jax.random.permutation(jax.random.fold_in(own, 3), count)
    donor, taker = mixed[0:count // 2 * 2:2], mixed[1:count // 2 * 2:2]
    margin = jnp.minimum(sizes[donor] - 1, reach - sizes[taker]) // 2
    margin = jnp.where((donor == sequence[0]) | (taker == sequence[0]) | (sizes[taker] == 0), 0, jnp.maximum(margin, 0))
    moved = jax.random.randint(jax.random.fold_in(own, 4), (count // 2,), 0, 1 << 20) % (margin + 1)
    sizes = sizes.at[donor].add(-moved).at[taker].add(moved)
    members = jnp.searchsorted(jnp.cumsum(sizes), jnp.arange(rows * top), side="right").astype(jnp.int32)
    grid = members.reshape(top, rows).T
    grid = grid[jax.random.permutation(jax.random.fold_in(own, 1), rows)]
    rotation = jax.random.randint(jax.random.fold_in(own, 2), (rows, 1), 0, top)
    return jnp.take_along_axis(grid, (jnp.arange(top)[None, :] + rotation) % top, axis=1)


def shares(amount, total, bound, lean, full):
    portions = [(1 << 20) // math.isqrt(rank ** lean) + 1 for rank in range(1, amount + 1)]
    largest = bound if full else min(bound, max(-(-total // amount), total * portions[0] // sum(portions)))
    least = 1 if total - largest >= amount - 1 else 0
    counts, spare = [largest] + [least] * (amount - 1), total - largest - least * (amount - 1)
    while spare > 0:
        free = [i for i in range(1, amount) if counts[i] < largest] or [i for i in range(1, amount) if counts[i] < bound]
        mass, left = sum([portions[i] for i in free]), spare
        for i in free:
            more = min(bound - counts[i], max(1, left * portions[i] // mass), spare)
            counts[i] = counts[i] + more
            spare = spare - more
    return np.array(counts)


def gaussian(rng, extent, scale, reach, cuts=(), kind=jnp.bfloat16):
    gain = steps_of(rng, extent, cuts, -0.22, 0.18) if cuts else 1.0
    values = jax.random.normal(rng, extent, jnp.float32) * scale * gain
    return jnp.minimum(jnp.maximum(values, -reach), reach).astype(kind)


def setup_inputs(seed: int = 0) -> dict:
    key_list = jax.random.split(jax.random.key(seed), 12)
    inputs = gaussian(key_list[0], (TOKENS, D), 1.0, 6.0, ((0, 32),))
    queries = draw_queries(jax.random.fold_in(key_list[11], 71), 0)
    keys = draw_keys(jax.random.fold_in(key_list[11], 71), 0)
    values = gaussian(key_list[3], (TOKENS, HD), 1.0, 6.0, ((0, 32),))
    norm_gain = jnp.clip(1.0 + 0.15 * jax.random.normal(key_list[4], (D,), jnp.float32), 0.25, 1.75)
    expert_ids_keys = jax.random.split(jax.random.fold_in(key_list[5], 1), TOKENS // TOK_DEV)
    expert_ids_turns = jax.random.permutation(jax.random.fold_in(key_list[5], 3), TOKENS // TOK_DEV)
    expert_ids = jax.vmap(lambda own, number: deal_out(jax.random.fold_in(key_list[5], 2), own, number, TOK_DEV, EXPERTS, TOP, CAP, 2))(expert_ids_keys, expert_ids_turns).reshape((TOKENS, TOP))
    gate_weights = jnp.clip(jnp.exp(math.log(1.0) - 1.609438 * jax.random.uniform(key_list[6], (TOKENS, TOP), jnp.float32) ** steps_of(key_list[6], (TOKENS, TOP), ((0, 32),), -0.2, 0.2)), 0.2, 1.0)
    pairs = draw_pairs(jax.random.fold_in(key_list[11], 71), 0)
    w_gate = gaussian(key_list[8], (EXPERTS, D, FF), D ** -0.5, 0.09375, ((0, 8), (2, 4)))
    w_up = gaussian(key_list[9], (EXPERTS, D, FF), D ** -0.5, 0.09375, ((0, 8), (2, 4)))
    w_down = gaussian(key_list[10], (EXPERTS, FF, D), FF ** -0.5, 0.09375, ((0, 8), (1, 4)))
    return {"inputs": inputs, "queries": queries, "keys": keys, "values": values, "norm_gain": norm_gain, "expert_ids": expert_ids, "gate_weights": gate_weights, "pairs": pairs, "w_gate": w_gate, "w_up": w_up, "w_down": w_down}


very_negative = -1e+30
norm_epsilon = 1e-05

def reference(inputs, queries, keys, values, norm_gain, expert_ids, gate_weights, pairs, w_gate, w_up, w_down):
    score_scale = 1.0 / math.sqrt(HSZ)
    block_ids = jnp.arange(NBLK, dtype=jnp.int32)
    slot_ids = jnp.arange(DIST + 1, dtype=jnp.int32)
    wanted_key = block_ids[:, None] - (DIST - slot_ids)[None, :]
    present_table = jnp.any((pairs[None, None, :, 0] == block_ids[:, None, None]) & (pairs[None, None, :, 1] == wanted_key[:, :, None]), axis=2)
    zero_rows = jnp.zeros((DIST * BLK, HD), keys.dtype)
    keys_ext = jnp.concatenate([zero_rows, keys], 0)
    values_ext = jnp.concatenate([zero_rows, values], 0)

    def attend_block(block_index):
        query_rows = lax.dynamic_slice_in_dim(queries, block_index * BLK, BLK, 0).astype(jnp.float32).reshape(BLK, HEADS, HSZ)
        key_rows = lax.dynamic_slice_in_dim(keys_ext, block_index * BLK, (DIST + 1) * BLK, 0).astype(jnp.float32).reshape(-1, HEADS, HSZ)
        value_rows = lax.dynamic_slice_in_dim(values_ext, block_index * BLK, (DIST + 1) * BLK, 0).astype(jnp.float32).reshape(-1, HEADS, HSZ)
        scores = jnp.einsum('qhd,khd->hqk', query_rows, key_rows) * score_scale
        key_mask = jnp.repeat(present_table[block_index], BLK)
        scores = jnp.where(key_mask[None, None, :], scores, very_negative)
        row_top = lax.optimization_barrier(jnp.max(scores, axis=2, keepdims=True))
        exp_scores = jnp.exp(scores - row_top)
        denominator = lax.optimization_barrier(jnp.sum(exp_scores, axis=2))
        weights = lax.optimization_barrier(exp_scores.astype(jnp.bfloat16)).astype(jnp.float32)
        summed = jnp.einsum('hqk,khd->qhd', weights, value_rows)
        return (summed / jnp.transpose(denominator)[:, :, None]).astype(jnp.bfloat16).reshape(BLK, HD)
    attended = lax.map(attend_block, block_ids).reshape(TOKENS, HD)
    mixed_sum = inputs.astype(jnp.float32) + attended.astype(jnp.float32)
    mean_square = lax.optimization_barrier(jnp.mean(mixed_sum * mixed_sum, axis=1, keepdims=True))
    normed = (mixed_sum * lax.rsqrt(mean_square + norm_epsilon) * norm_gain[None, :]).astype(jnp.bfloat16)
    flat_ids = expert_ids.reshape(-1)
    per_expert = TOKENS * TOP // EXPERTS

    def serve(expert):
        chosen = jnp.argsort((flat_ids != expert).astype(jnp.int32), stable=True)[:per_expert].astype(jnp.int32)
        token_rows = normed[chosen // TOP]
        gate_value = jnp.dot(token_rows, w_gate[expert], preferred_element_type=jnp.float32)
        up_value = jnp.dot(token_rows, w_up[expert], preferred_element_type=jnp.float32)
        hidden = (jax.nn.silu(gate_value) * up_value).astype(jnp.bfloat16)
        running_sum = jnp.zeros((per_expert, D), jnp.float32)
        for run_index in range(N_SEQ):
            partial_value = jnp.dot(hidden[:, run_index * FFSLICE:(run_index + 1) * FFSLICE], w_down[expert, run_index * FFSLICE:(run_index + 1) * FFSLICE], preferred_element_type=jnp.float32)
            partial_value = lax.optimization_barrier(partial_value.astype(jnp.bfloat16))
            running_sum = running_sum + partial_value.astype(jnp.float32)
        return (chosen, running_sum)
    chosen_all, out_all = lax.map(serve, jnp.arange(EXPERTS, dtype=jnp.int32))
    contrib = jnp.zeros((TOKENS * TOP, D), jnp.float32).at[chosen_all.reshape(-1)].set(out_all.reshape(-1, D))
    contrib = contrib.reshape(TOKENS, TOP, D)
    output = mixed_sum + lax.optimization_barrier(jnp.sum(gate_weights[:, :, None] * contrib, axis=1))
    return output.astype(jnp.bfloat16)
```

```python
import functools
import math

import jax
import jax.numpy as jnp
from jax import lax
from jax.experimental import pallas as pl
from jax.experimental.pallas import tpu as pltpu
from jax.sharding import PartitionSpec as P

HSZ = 128
TOP = 2
BLK = 512
DIST = 2
OUTER = 2
AHEAD = 2

very_negative = -1e30
norm_epsilon = 1e-05

MESH = pl.DeviceIdType.MESH
ANY = pl.BlockSpec(memory_space=pl.ANY)
DMA = pltpu.SemaphoreType.DMA


def remote(source, target, send_sem, recv_sem, device):
    return pltpu.make_async_remote_copy(
        src_ref=source,
        dst_ref=target,
        send_sem=send_sem,
        recv_sem=recv_sem,
        device_id=device,
        device_id_type=MESH,
    )


def enter(peers):
    barrier = pltpu.get_barrier_semaphore()
    for peer in peers:
        pl.semaphore_signal(barrier, inc=1, device_id=peer, device_id_type=MESH)
    pl.semaphore_wait(barrier, len(peers))


def turned(index, steps, count):
    return lax.rem(index + (steps % count), count)


def params(collective_id, vmem=None):
    return pltpu.CompilerParams(
        collective_id=collective_id, has_side_effects=True, vmem_limit_bytes=vmem
    )


def qkv_kernel(
    seq_count, exp_count, tail, q_ref, k_ref, v_ref, qr_ref, kx_ref, vx_ref,
    local_sem, z_send, z_recv, f_send, f_recv,
):
    s, e = lax.axis_index("seq"), lax.axis_index("exp")
    rows = q_ref.shape[0]
    group = qr_ref.shape[1]
    run = qr_ref.shape[0]
    arrays = ((k_ref, kx_ref, tail), (v_ref, vx_ref, tail), (q_ref, qr_ref, 0))
    enter(
        [(s, turned(e, k, exp_count)) for k in range(1, exp_count)]
        + [(turned(s, 1, seq_count), e), (turned(s, -1, seq_count), e)]
    )

    def columns(ref, index):
        return ref.at[:, pl.ds(pl.multiple_of(index * group, group), group)]

    def lines(ref, offset, index):
        return ref.at[pl.ds(pl.multiple_of(offset + index * rows, rows), rows)]

    waits = []
    for i, (source, target, offset) in enumerate(arrays):
        for k in range(1, exp_count):
            d = turned(e, k, exp_count)
            copy = remote(
                columns(source, d), lines(target, offset, e), z_send.at[i, k], z_recv.at[i, k], (s, d)
            )
            copy.start()
            waits.append(copy)
    locals_ = []
    for i, (source, target, offset) in enumerate(arrays):
        copy = pltpu.make_async_copy(columns(source, e), lines(target, offset, e), local_sem.at[i])
        copy.start()
        locals_.append(copy)

    def relay(i, k, act):
        source, target, offset = arrays[i]
        c = turned(e, -k, exp_count)
        inside = (c + 1) * rows > run - tail
        block = columns(source, e) if k == 0 else lines(target, offset, c)
        row = pl.multiple_of(lax.max(c * rows - (run - tail), 0), rows)
        copy = remote(
            block, target.at[pl.ds(row, rows)], f_send.at[i, k], f_recv.at[i, k],
            (turned(s, 1, seq_count), e),
        )
        if act == "start":
            pl.when(inside & (s < seq_count - 1))(copy.start)
        elif act == "send":
            pl.when(inside & (s < seq_count - 1))(copy.wait_send)
        else:
            pl.when(inside & (s > 0))(copy.wait_recv)

    for i in range(3):
        for k in range(exp_count):
            if k > 0:
                source, target, offset = arrays[i]
                block = lines(target, offset, turned(e, -k, exp_count))
                remote(block, block, z_send.at[i, k], z_recv.at[i, k], (s, e)).wait_recv()
            if i < 2:
                relay(i, k, "start")
    for i in range(2):
        for k in range(exp_count):
            relay(i, k, "recv")
            relay(i, k, "send")
    for copy in waits:
        copy.wait_send()
    for copy in locals_:
        copy.wait()


def exchange_qkv(queries, keys, values, seq_count, exp_count, tail):
    rows, width = queries.shape
    group, run = width // exp_count, rows * exp_count
    kind = queries.dtype
    return pl.pallas_call(
        functools.partial(qkv_kernel, seq_count, exp_count, tail),
        out_shape=(
            jax.ShapeDtypeStruct((run, group), kind),
            jax.ShapeDtypeStruct((tail + run, group), kind),
            jax.ShapeDtypeStruct((tail + run, group), kind),
        ),
        in_specs=[ANY] * 3,
        out_specs=(ANY,) * 3,
        scratch_shapes=[
            DMA((3,)),
            DMA((3, exp_count)),
            DMA((3, exp_count)),
            DMA((2, exp_count)),
            DMA((2, exp_count)),
        ],
        compiler_params=params(1),
        name="qkv_exchange",
    )(queries, keys, values)


def attend_kernel(slots, present_ref, q_ref, *refs):
    k_refs, v_refs, o_ref = refs[:slots], refs[slots : 2 * slots], refs[2 * slots]
    block = pl.program_id(0)
    scale = 1.0 / math.sqrt(q_ref.shape[1])
    q = q_ref[...]
    scores = []
    for j in range(slots):
        score = lax.dot_general(
            q, k_refs[j][...], (((1,), (1,)), ((), ())), preferred_element_type=jnp.float32
        )
        scores.append(jnp.where(present_ref[block, j] > 0, score * scale, very_negative))
    top = functools.reduce(jnp.maximum, [jnp.max(x, axis=1, keepdims=True) for x in scores])
    total, summed = 0.0, 0.0
    for j in range(slots):
        exps = jnp.exp(scores[j] - top)
        total = total + jnp.sum(exps, axis=1, keepdims=True)
        value = v_refs[j][...]
        value = jnp.where(present_ref[block, j] > 0, value, jnp.zeros_like(value))
        summed = summed + jnp.dot(
            exps.astype(jnp.bfloat16), value, preferred_element_type=jnp.float32
        )
    o_ref[...] = (summed / total).astype(o_ref.dtype)


def attend(query_run, keys_ext, values_ext, present):
    run, group = query_run.shape
    slots = present.shape[1]

    def at(slot):
        return pl.BlockSpec((BLK, HSZ), lambda block, head, flags: (block + slot, head))

    return pl.pallas_call(
        functools.partial(attend_kernel, slots),
        out_shape=jax.ShapeDtypeStruct((run, group), query_run.dtype),
        grid_spec=pltpu.PrefetchScalarGridSpec(
            num_scalar_prefetch=1,
            grid=(run // BLK, group // HSZ),
            in_specs=[at(0)] + [at(j) for j in range(slots)] * 2,
            out_specs=at(0),
        ),
        name="attend",
    )(present, query_run, *([keys_ext] * slots), *([values_ext] * slots))


def back_kernel(exp_count, a_ref, o_ref, local_sem, z_send, z_recv):
    s, e = lax.axis_index("seq"), lax.axis_index("exp")
    rows, group = o_ref.shape[0], a_ref.shape[1]
    enter([(s, turned(e, k, exp_count)) for k in range(1, exp_count)])

    def lines(index):
        return a_ref.at[pl.ds(pl.multiple_of(index * rows, rows), rows)]

    def columns(index):
        return o_ref.at[:, pl.ds(pl.multiple_of(index * group, group), group)]

    copies = []
    for k in range(1, exp_count):
        d = turned(e, k, exp_count)
        copy = remote(lines(d), columns(e), z_send.at[k], z_recv.at[k], (s, d))
        copy.start()
        copies.append(copy)
    own = pltpu.make_async_copy(lines(e), columns(e), local_sem)
    own.start()
    for k in range(1, exp_count):
        block = columns(turned(e, -k, exp_count))
        remote(block, block, z_send.at[k], z_recv.at[k], (s, e)).wait_recv()
    for copy in copies:
        copy.wait_send()
    own.wait()


def exchange_back(attended_run, exp_count):
    run, group = attended_run.shape
    return pl.pallas_call(
        functools.partial(back_kernel, exp_count),
        out_shape=jax.ShapeDtypeStruct((run // exp_count, group * exp_count), attended_run.dtype),
        in_specs=[ANY],
        out_specs=ANY,
        scratch_shapes=[DMA, DMA((exp_count,)), DMA((exp_count,))],
        compiler_params=params(2),
        name="attended_back",
    )(attended_run)


def dispatch_kernel(
    seq_count, exp_count, out_ref, rows_ref, local_sem, z_send, z_recv, x_send, x_recv, d_send, d_recv
):
    s, e = lax.axis_index("seq"), lax.axis_index("exp")
    inner_count = seq_count // OUTER
    half = out_ref.shape[2] // 2
    a, b = lax.div(s, inner_count), lax.rem(s, inner_count)
    outer = (1 - a) * inner_count + b
    forth = [a * inner_count + turned(b, j, inner_count) for j in range(1, inner_count)]
    back = [a * inner_count + turned(b, -j, inner_count) for j in range(1, inner_count)]
    across = [(1 - a) * inner_count + turned(b, -j, inner_count) for j in range(1, inner_count)]
    peers = [outer] + forth
    sources = [outer] + back
    enter(
        [(s, turned(e, k, exp_count)) for k in range(1, exp_count)] + [(p, e) for p in peers]
    )
    copies = []

    def start(copy):
        copy.start()
        copies.append(copy)

    def arrived(block, send_sem, recv_sem):
        remote(block, block, send_sem, recv_sem, (s, e)).wait_recv()

    for k in range(1, exp_count):
        d = turned(e, k, exp_count)
        start(remote(out_ref.at[d], rows_ref.at[s, e], z_send.at[k], z_recv.at[k], (s, d)))
    own = pltpu.make_async_copy(out_ref.at[e], rows_ref.at[s, e], local_sem)
    own.start()
    low, high = pl.ds(0, half), pl.ds(half, half)
    for k in range(exp_count + 1):
        if k < exp_count:
            c = turned(e, -k, exp_count)
            if k > 0:
                arrived(rows_ref.at[s, c], z_send.at[k], z_recv.at[k])
            block = out_ref.at[e] if k == 0 else rows_ref.at[s, c]
            for i, p in enumerate(peers):
                start(remote(block, rows_ref.at[s, c], x_send.at[i, k], x_recv.at[i, k], (p, e)))
        if k > 0:
            n = k - 1
            c = turned(e, -n, exp_count)
            for i, source in enumerate(sources):
                arrived(rows_ref.at[source, c], x_send.at[i, n], x_recv.at[i, n])
                if i == 0:
                    block = rows_ref.at[source, c, :, low]
                    for j, p in enumerate(forth):
                        start(remote(block, block, d_send.at[0, j, n], d_recv.at[0, j, n], (p, e)))
                else:
                    block = rows_ref.at[source, c, :, high]
                    start(
                        remote(block, block, d_send.at[1, i - 1, n], d_recv.at[1, i - 1, n], (outer, e))
                    )
    for n in range(exp_count):
        c = turned(e, -n, exp_count)
        for j, source in enumerate(across):
            for h, part in enumerate((low, high)):
                arrived(rows_ref.at[source, c, :, part], d_send.at[h, j, n], d_recv.at[h, j, n])
    for copy in copies:
        copy.wait_send()
    own.wait()


def dispatch(outgoing, seq_count, exp_count):
    inner_count = seq_count // OUTER
    return pl.pallas_call(
        functools.partial(dispatch_kernel, seq_count, exp_count),
        out_shape=jax.ShapeDtypeStruct((seq_count,) + outgoing.shape, outgoing.dtype),
        in_specs=[ANY],
        out_specs=ANY,
        scratch_shapes=[
            DMA,
            DMA((exp_count,)),
            DMA((exp_count,)),
            DMA((inner_count, exp_count)),
            DMA((inner_count, exp_count)),
            DMA((2, max(1, inner_count - 1), exp_count)),
            DMA((2, max(1, inner_count - 1), exp_count)),
        ],
        compiler_params=params(3),
        name="dispatch",
    )(outgoing)


def collect_kernel(
    seq_count, exp_count, y_ref, got_ref, own0, own1, in0, in1, out0, out1, keep0, keep1, mid0, mid1, done,
    own_sem, p_send, p_recv, m_send, m_recv, z_send, z_recv, local_sem,
):
    s, e = lax.axis_index("seq"), lax.axis_index("exp")
    inner_count = seq_count // OUTER
    half = y_ref.shape[4] // 2
    a, b = lax.div(s, inner_count), lax.rem(s, inner_count)
    other = 1 - a
    outer = other * inner_count + b
    forth = [turned(b, j, inner_count) for j in range(1, inner_count)]
    enter(
        [(s, turned(e, k, exp_count)) for k in range(1, exp_count)]
        + [(outer, e)]
        + [(a * inner_count + f, e) for f in forth]
    )
    low, high = pl.ds(0, half), pl.ds(half, half)
    copies = []

    def start(copy):
        copy.start()
        copies.append(copy)

    def arrived(block, send_sem, recv_sem):
        remote(block, block, send_sem, recv_sem, (s, e)).wait_recv()

    def chunk(k):
        return turned(e, k + 1, exp_count)

    def loads(k):
        c = chunk(k)
        return (
            pltpu.make_async_copy(y_ref.at[:, b, c, :, low], own0.at[k], own_sem.at[0, k]),
            pltpu.make_async_copy(y_ref.at[a, :, c, :, high], own1.at[k], own_sem.at[1, k]),
        )

    def first(k):
        c = chunk(k)
        start(
            remote(y_ref.at[other, :, c, :, high], in1.at[k], p_send.at[0, k], p_recv.at[0, k], (outer, e))
        )
        for j, f in enumerate(forth):
            start(
                remote(
                    y_ref.at[:, f, c, :, low], in0.at[j, k], p_send.at[1 + j, k], p_recv.at[1 + j, k],
                    (a * inner_count + f, e),
                )
            )
        for load in loads(k):
            load.start()

    def wide(ref, *index):
        return ref[index].astype(jnp.float32)

    def second(k):
        for load in loads(k):
            load.wait()
        for j in range(inner_count - 1):
            arrived(in0.at[j, k], p_send.at[1 + j, k], p_recv.at[1 + j, k])
        out0[k] = sum([wide(in0, j, k, other) for j in range(inner_count - 1)], wide(own0, k, other)).astype(
            out0.dtype
        )
        start(remote(out0.at[k], mid0.at[k], m_send.at[0, k], m_recv.at[0, k], (outer, e)))
        arrived(in1.at[k], p_send.at[0, k], p_recv.at[0, k])
        for j, f in enumerate(forth):
            out1[j, k] = (wide(own1, k, f) + wide(in1, k, f)).astype(out1.dtype)
            start(
                remote(
                    out1.at[j, k], mid1.at[j, k], m_send.at[1 + j, k], m_recv.at[1 + j, k],
                    (a * inner_count + f, e),
                )
            )
        keep0[k] = sum([wide(in0, j, k, a) for j in range(inner_count - 1)], wide(own0, k, a))
        keep1[k] = wide(own1, k, b) + wide(in1, k, b)

    def third(k):
        arrived(mid0.at[k], m_send.at[0, k], m_recv.at[0, k])
        done[k, :, low] = (keep0[k] + wide(mid0, k)).astype(done.dtype)
        for j in range(inner_count - 1):
            arrived(mid1.at[j, k], m_send.at[1 + j, k], m_recv.at[1 + j, k])
        done[k, :, high] = sum(
            [wide(mid1, j, k) for j in range(inner_count - 1)], keep1[k]
        ).astype(done.dtype)
        if k < exp_count - 1:
            start(remote(done.at[k], got_ref.at[e], z_send.at[k], z_recv.at[k], (s, chunk(k))))
        else:
            pltpu.make_async_copy(done.at[k], got_ref.at[e], local_sem).start()

    for k in range(min(AHEAD, exp_count)):
        first(k)
    for k in range(exp_count + 1):
        if k + AHEAD < exp_count:
            first(k + AHEAD)
        if k < exp_count:
            second(k)
        if k > 0:
            third(k - 1)
    for k in range(exp_count - 1):
        arrived(got_ref.at[turned(e, -k - 1, exp_count)], z_send.at[k], z_recv.at[k])
    for copy in copies:
        copy.wait_send()
    pltpu.make_async_copy(done.at[exp_count - 1], got_ref.at[e], local_sem).wait()


def collect(partials, seq_count, exp_count):
    capacity, width = partials.shape[2:]
    inner_count = seq_count // OUTER
    inner_peers = inner_count - 1
    half = width // 2
    kind = partials.dtype
    return pl.pallas_call(
        functools.partial(collect_kernel, seq_count, exp_count),
        out_shape=jax.ShapeDtypeStruct((exp_count, capacity, width), kind),
        in_specs=[ANY],
        out_specs=ANY,
        scratch_shapes=[
            pltpu.VMEM((exp_count, OUTER, capacity, half), kind),
            pltpu.VMEM((exp_count, inner_count, capacity, half), kind),
            pltpu.VMEM((inner_peers, exp_count, OUTER, capacity, half), kind),
            pltpu.VMEM((exp_count, inner_count, capacity, half), kind),
            pltpu.VMEM((exp_count, capacity, half), kind),
            pltpu.VMEM((inner_peers, exp_count, capacity, half), kind),
            pltpu.VMEM((exp_count, capacity, half), jnp.float32),
            pltpu.VMEM((exp_count, capacity, half), jnp.float32),
            pltpu.VMEM((exp_count, capacity, half), kind),
            pltpu.VMEM((inner_peers, exp_count, capacity, half), kind),
            pltpu.VMEM((exp_count, capacity, width), kind),
            DMA((2, exp_count)),
            DMA((inner_count, exp_count)),
            DMA((inner_count, exp_count)),
            DMA((inner_count, exp_count)),
            DMA((inner_count, exp_count)),
            DMA((exp_count,)),
            DMA((exp_count,)),
            DMA,
        ],
        compiler_params=params(4, 48 * 1024 * 1024),
        name="collect",
    )(partials.reshape(OUTER, inner_count, exp_count, capacity, width))


def expert_part(flat_rows, gate_slice, up_slice, down_slice):
    gate_value = jnp.dot(flat_rows, gate_slice, preferred_element_type=jnp.float32)
    up_value = jnp.dot(flat_rows, up_slice, preferred_element_type=jnp.float32)
    hidden = (jax.nn.silu(gate_value) * up_value).astype(jnp.bfloat16)
    return jnp.dot(hidden, down_slice, preferred_element_type=jnp.float32)


def per_device(
    inputs, queries, keys, values, norm_gain, expert_ids, gate_weights, pairs, w_gate, w_up, w_down
):
    rows_dev, model_width = inputs.shape
    seq_count, exp_count = lax.axis_size("seq"), lax.axis_size("exp")
    query_run, keys_ext, values_ext = exchange_qkv(
        queries, keys, values, seq_count, exp_count, DIST * BLK
    )
    blocks_dev = query_run.shape[0] // BLK
    query_block = lax.axis_index("seq") * blocks_dev + jnp.arange(blocks_dev, dtype=jnp.int32)
    key_block = query_block[:, None] - (DIST - jnp.arange(DIST + 1, dtype=jnp.int32))[None, :]
    present = jnp.any(
        (pairs[None, None, :, 0] == query_block[:, None, None])
        & (pairs[None, None, :, 1] == key_block[:, :, None]),
        axis=2,
    ).astype(jnp.int32)
    attended = exchange_back(attend(query_run, keys_ext, values_ext, present), exp_count)
    mixed_sum = inputs.astype(jnp.float32) + attended.astype(jnp.float32)
    mean_square = jnp.mean(mixed_sum * mixed_sum, axis=1, keepdims=True)
    normed = (mixed_sum * lax.rsqrt(mean_square + norm_epsilon) * norm_gain[None, :]).astype(
        jnp.bfloat16
    )
    capacity = rows_dev * TOP // exp_count
    places = exp_count * capacity
    flat_ids = expert_ids.reshape(-1)
    id_table = (flat_ids[:, None] == jnp.arange(exp_count, dtype=jnp.int32)[None, :]).astype(
        jnp.int32
    )
    ahead_count = jnp.cumsum(id_table, axis=0) - id_table
    position = jnp.sum(ahead_count * id_table, axis=1)
    target = (flat_ids * capacity + position).reshape(rows_dev, TOP)
    slots = jnp.arange(places, dtype=jnp.int32)
    spots = target[:, :, None] == slots[None, None, :]
    choose = jnp.any(spots, axis=1).astype(jnp.bfloat16)
    outgoing = (
        lax.dot_general(choose, normed, (((0,), (0,)), ((), ())), preferred_element_type=jnp.float32)
        .astype(jnp.bfloat16)
        .reshape(exp_count, capacity, model_width)
    )
    piece_rows = dispatch(outgoing, seq_count, exp_count)
    parts = expert_part(piece_rows.reshape(-1, model_width), w_gate[0], w_up[0], w_down[0])
    got = collect(parts.astype(jnp.bfloat16).reshape(piece_rows.shape), seq_count, exp_count)
    weight = jnp.sum(jnp.where(spots, gate_weights[:, :, None], 0.0), axis=1)
    coarse = weight.astype(jnp.bfloat16)
    fine = (weight - coarse.astype(jnp.float32)).astype(jnp.bfloat16)
    flat = got.reshape(places, model_width)
    combined = jnp.dot(coarse, flat, preferred_element_type=jnp.float32) + jnp.dot(
        fine, flat, preferred_element_type=jnp.float32
    )
    return (mixed_sum + combined).astype(jnp.bfloat16)


def solution(mesh):
    rows = P(("seq", "exp"), None)
    in_specs = (
        rows, rows, rows, rows, P(), rows, rows, P(),
        P("exp", None, "seq"), P("exp", None, "seq"), P("exp", "seq", None),
    )
    return jax.shard_map(
        per_device, mesh=mesh, in_specs=in_specs, out_specs=rows, check_vma=False
    )
```

```python
import functools
import math

import jax
import jax.numpy as jnp
from jax import lax
from jax.experimental import pallas as pl
from jax.experimental.pallas import tpu as pltpu
from jax.sharding import PartitionSpec as P

HSZ = 128
TOP = 2
BLK = 512
DIST = 2
OUTER = 2

very_negative = -1e30
norm_epsilon = 1e-05

MESH = pl.DeviceIdType.MESH
ANY = pl.BlockSpec(memory_space=pl.ANY)
DMA = pltpu.SemaphoreType.DMA


def remote(source, target, send_sem, recv_sem, device):
    return pltpu.make_async_remote_copy(
        src_ref=source,
        dst_ref=target,
        send_sem=send_sem,
        recv_sem=recv_sem,
        device_id=device,
        device_id_type=MESH,
    )


def enter(peers):
    barrier = pltpu.get_barrier_semaphore()
    for peer in peers:
        pl.semaphore_signal(barrier, inc=1, device_id=peer, device_id_type=MESH)
    pl.semaphore_wait(barrier, len(peers))


def turned(index, steps, count):
    return lax.rem(index + (steps % count), count)


def params(collective_id, vmem=None):
    return pltpu.CompilerParams(
        collective_id=collective_id, has_side_effects=True, vmem_limit_bytes=vmem
    )


def qkv_kernel(
    seq_count, exp_count, tail, q_ref, k_ref, v_ref, qr_ref, kx_ref, vx_ref,
    local_sem, z_send, z_recv, f_send, f_recv,
):
    s, e = lax.axis_index("seq"), lax.axis_index("exp")
    rows = q_ref.shape[0]
    group = qr_ref.shape[1]
    run = qr_ref.shape[0]
    arrays = ((k_ref, kx_ref, tail), (v_ref, vx_ref, tail), (q_ref, qr_ref, 0))
    enter(
        [(s, turned(e, k, exp_count)) for k in range(1, exp_count)]
        + [(turned(s, 1, seq_count), e), (turned(s, -1, seq_count), e)]
    )

    def columns(ref, index):
        return ref.at[:, pl.ds(pl.multiple_of(index * group, group), group)]

    def lines(ref, offset, index):
        return ref.at[pl.ds(pl.multiple_of(offset + index * rows, rows), rows)]

    waits = []
    for i, (source, target, offset) in enumerate(arrays):
        for k in range(1, exp_count):
            d = turned(e, k, exp_count)
            copy = remote(
                columns(source, d), lines(target, offset, e), z_send.at[i, k], z_recv.at[i, k], (s, d)
            )
            copy.start()
            waits.append(copy)
    locals_ = []
    for i, (source, target, offset) in enumerate(arrays):
        copy = pltpu.make_async_copy(columns(source, e), lines(target, offset, e), local_sem.at[i])
        copy.start()
        locals_.append(copy)

    def relay(i, k, act):
        source, target, offset = arrays[i]
        c = turned(e, -k, exp_count)
        inside = (c + 1) * rows > run - tail
        block = columns(source, e) if k == 0 else lines(target, offset, c)
        row = pl.multiple_of(lax.max(c * rows - (run - tail), 0), rows)
        copy = remote(
            block, target.at[pl.ds(row, rows)], f_send.at[i, k], f_recv.at[i, k],
            (turned(s, 1, seq_count), e),
        )
        if act == "start":
            pl.when(inside & (s < seq_count - 1))(copy.start)
        elif act == "send":
            pl.when(inside & (s < seq_count - 1))(copy.wait_send)
        else:
            pl.when(inside & (s > 0))(copy.wait_recv)

    for i in range(3):
        for k in range(exp_count):
            if k > 0:
                source, target, offset = arrays[i]
                block = lines(target, offset, turned(e, -k, exp_count))
                remote(block, block, z_send.at[i, k], z_recv.at[i, k], (s, e)).wait_recv()
            if i < 2:
                relay(i, k, "start")
    for i in range(2):
        for k in range(exp_count):
            relay(i, k, "recv")
            relay(i, k, "send")
    for copy in waits:
        copy.wait_send()
    for copy in locals_:
        copy.wait()


def exchange_qkv(queries, keys, values, seq_count, exp_count, tail):
    rows, width = queries.shape
    group, run = width // exp_count, rows * exp_count
    kind = queries.dtype
    return pl.pallas_call(
        functools.partial(qkv_kernel, seq_count, exp_count, tail),
        out_shape=(
            jax.ShapeDtypeStruct((run, group), kind),
            jax.ShapeDtypeStruct((tail + run, group), kind),
            jax.ShapeDtypeStruct((tail + run, group), kind),
        ),
        in_specs=[ANY] * 3,
        out_specs=(ANY,) * 3,
        scratch_shapes=[
            DMA((3,)),
            DMA((3, exp_count)),
            DMA((3, exp_count)),
            DMA((2, exp_count)),
            DMA((2, exp_count)),
        ],
        compiler_params=params(1),
        name="qkv_exchange",
    )(queries, keys, values)


def attend_kernel(slots, present_ref, q_ref, *refs):
    k_refs, v_refs, o_ref = refs[:slots], refs[slots : 2 * slots], refs[2 * slots]
    block = pl.program_id(0)
    scale = 1.0 / math.sqrt(q_ref.shape[1])
    q = q_ref[...]
    scores = []
    for j in range(slots):
        score = lax.dot_general(
            q, k_refs[j][...], (((1,), (1,)), ((), ())), preferred_element_type=jnp.float32
        )
        scores.append(jnp.where(present_ref[block, j] > 0, score * scale, very_negative))
    top = functools.reduce(jnp.maximum, [jnp.max(x, axis=1, keepdims=True) for x in scores])
    total, summed = 0.0, 0.0
    for j in range(slots):
        exps = jnp.exp(scores[j] - top)
        total = total + jnp.sum(exps, axis=1, keepdims=True)
        value = v_refs[j][...]
        value = jnp.where(present_ref[block, j] > 0, value, jnp.zeros_like(value))
        summed = summed + jnp.dot(
            exps.astype(jnp.bfloat16), value, preferred_element_type=jnp.float32
        )
    o_ref[...] = (summed / total).astype(o_ref.dtype)


def attend(query_run, keys_ext, values_ext, present):
    run, group = query_run.shape
    slots = present.shape[1]

    def at(slot):
        return pl.BlockSpec((BLK, HSZ), lambda block, head, flags: (block + slot, head))

    return pl.pallas_call(
        functools.partial(attend_kernel, slots),
        out_shape=jax.ShapeDtypeStruct((run, group), query_run.dtype),
        grid_spec=pltpu.PrefetchScalarGridSpec(
            num_scalar_prefetch=1,
            grid=(run // BLK, group // HSZ),
            in_specs=[at(0)] + [at(j) for j in range(slots)] * 2,
            out_specs=at(0),
        ),
        name="attend",
    )(present, query_run, *([keys_ext] * slots), *([values_ext] * slots))


def back_kernel(exp_count, a_ref, o_ref, local_sem, z_send, z_recv):
    s, e = lax.axis_index("seq"), lax.axis_index("exp")
    rows, group = o_ref.shape[0], a_ref.shape[1]
    enter([(s, turned(e, k, exp_count)) for k in range(1, exp_count)])

    def lines(index):
        return a_ref.at[pl.ds(pl.multiple_of(index * rows, rows), rows)]

    def columns(index):
        return o_ref.at[:, pl.ds(pl.multiple_of(index * group, group), group)]

    copies = []
    for k in range(1, exp_count):
        d = turned(e, k, exp_count)
        copy = remote(lines(d), columns(e), z_send.at[k], z_recv.at[k], (s, d))
        copy.start()
        copies.append(copy)
    own = pltpu.make_async_copy(lines(e), columns(e), local_sem)
    own.start()
    for k in range(1, exp_count):
        block = columns(turned(e, -k, exp_count))
        remote(block, block, z_send.at[k], z_recv.at[k], (s, e)).wait_recv()
    for copy in copies:
        copy.wait_send()
    own.wait()


def exchange_back(attended_run, exp_count):
    run, group = attended_run.shape
    return pl.pallas_call(
        functools.partial(back_kernel, exp_count),
        out_shape=jax.ShapeDtypeStruct((run // exp_count, group * exp_count), attended_run.dtype),
        in_specs=[ANY],
        out_specs=ANY,
        scratch_shapes=[DMA, DMA((exp_count,)), DMA((exp_count,))],
        compiler_params=params(2),
        name="attended_back",
    )(attended_run)


def experts_kernel(
    seq_count, exp_count, together, tile, wide_tile,
    out_ref, gate_hbm, up_hbm, down_hbm, got_ref,
    gate_ref, up_ref, down_ref, buf, x_ref, hid_ref, in0, in1, out0, out1, mid0, mid1, done,
    local_sem, w_sem, z_send, z_recv, x_send, x_recv, d_send, d_recv,
    p_send, p_recv, m_send, m_recv, g_send, g_recv,
):
    s, e = lax.axis_index("seq"), lax.axis_index("exp")
    inner_count = seq_count // OUTER
    capacity, width = out_ref.shape[1:]
    half = width // 2
    a, b = lax.div(s, inner_count), lax.rem(s, inner_count)
    other = 1 - a
    outer = (other * inner_count + b, e)
    steps = range(1, inner_count)
    forth = [turned(b, j, inner_count) for j in steps]
    back = [turned(b, -j, inner_count) for j in steps]
    inner = [(a * inner_count + f, e) for f in forth]
    low, high = pl.ds(0, half), pl.ds(half, half)
    groups = exp_count // together
    chunk_rows = seq_count * capacity

    def chunk(k):
        return lax.rem(e - k + exp_count, exp_count)

    def arrived(block, send_sem, recv_sem):
        remote(block, block, send_sem, recv_sem, (s, e)).wait_recv()

    weights = [
        pltpu.make_async_copy(source.at[0], target, w_sem.at[i])
        for i, (source, target) in enumerate(
            ((gate_hbm, gate_ref), (up_hbm, up_ref), (down_hbm, down_ref))
        )
    ]
    own = pltpu.make_async_copy(out_ref.at[e], buf.at[a, b, e], local_sem)
    own.start()
    enter([(s, turned(e, k, exp_count)) for k in range(1, exp_count)] + [outer] + inner)

    def spread(k):
        d = lax.rem(e + k, exp_count)
        return remote(out_ref.at[d], buf.at[a, b, e], z_send.at[k], z_recv.at[k], (s, d))

    def directs(k):
        block = buf.at[a, b, chunk(k)]
        return [
            remote(block, block, x_send.at[i, k], x_recv.at[i, k], peer)
            for i, peer in enumerate([outer] + inner)
        ]

    def relays(k):
        c = chunk(k)
        copies = []
        for j, peer in enumerate(inner):
            block = buf.at[other, b, c, :, low]
            copies.append(remote(block, block, d_send.at[0, j, k], d_recv.at[0, j, k], peer))
            block = buf.at[a, back[j], c, :, high]
            copies.append(remote(block, block, d_send.at[1, j, k], d_recv.at[1, j, k], outer))
        return copies

    def gather_step(k):
        @pl.when(k < exp_count)
        def _():
            @pl.when(k > 0)
            def _():
                arrived(buf.at[a, b, chunk(k)], z_send.at[k], z_recv.at[k])

            for copy in directs(k):
                copy.start()

        @pl.when((k > 0) & (k <= exp_count))
        def _():
            n = k - 1
            c = chunk(n)
            arrived(buf.at[other, b, c], x_send.at[0, n], x_recv.at[0, n])
            for j in range(inner_count - 1):
                arrived(buf.at[a, back[j], c], x_send.at[1 + j, n], x_recv.at[1 + j, n])
            for copy in relays(n):
                copy.start()

    def complete(k):
        c = chunk(k)
        for j in range(inner_count - 1):
            for h, part in enumerate((low, high)):
                arrived(buf.at[other, back[j], c, :, part], d_send.at[h, j, k], d_recv.at[h, j, k])

    def first(k):
        c = chunk(k)
        return [
            remote(buf.at[other, :, c, :, high], in1.at[k], p_send.at[0, k], p_recv.at[0, k], outer)
        ] + [
            remote(
                buf.at[:, f, c, :, low], in0.at[j, k], p_send.at[1 + j, k], p_recv.at[1 + j, k], inner[j]
            )
            for j, f in enumerate(forth)
        ]

    def second(k):
        return [remote(out0.at[k], mid0.at[k], m_send.at[0, k], m_recv.at[0, k], outer)] + [
            remote(out1.at[j, k], mid1.at[j, k], m_send.at[1 + j, k], m_recv.at[1 + j, k], inner[j])
            for j in range(inner_count - 1)
        ]

    def third(k):
        return remote(done.at[k], got_ref.at[e], g_send.at[k], g_recv.at[k], (s, chunk(k)))

    def stay():
        return pltpu.make_async_copy(done.at[0], got_ref.at[e], local_sem)

    def wide(value):
        return value.astype(jnp.float32)

    def inner_sum(k, side):
        total = wide(buf[side, b, chunk(k), :, low])
        for j in range(inner_count - 1):
            total = total + wide(in0[j, k, side])
        return total

    def outer_sum(k, lane):
        return wide(buf[a, lane, chunk(k), :, high]) + wide(in1[k, lane])

    def sum_step(k):
        @pl.when((k >= 0) & (k < exp_count))
        def _():
            sends = second(k)
            for j in range(inner_count - 1):
                arrived(in0.at[j, k], p_send.at[1 + j, k], p_recv.at[1 + j, k])
            out0[k] = inner_sum(k, other).astype(out0.dtype)
            sends[0].start()
            arrived(in1.at[k], p_send.at[0, k], p_recv.at[0, k])
            for j, f in enumerate(forth):
                out1[j, k] = outer_sum(k, f).astype(out1.dtype)
                sends[1 + j].start()

        @pl.when((k > 0) & (k <= exp_count))
        def _():
            n = k - 1
            arrived(mid0.at[n], m_send.at[0, n], m_recv.at[0, n])
            done[n, :, low] = (inner_sum(n, a) + wide(mid0[n])).astype(done.dtype)
            total = outer_sum(n, b)
            for j in range(inner_count - 1):
                arrived(mid1.at[j, n], m_send.at[1 + j, n], m_recv.at[1 + j, n])
                total = total + wide(mid1[j, n])
            done[n, :, high] = total.astype(done.dtype)

            @pl.when(n == 0)
            def _():
                stay().start()

            @pl.when(n > 0)
            def _():
                third(n).start()

    def loop(begin, end, body):
        def step(i, carry):
            body(i)
            return carry

        lax.fori_loop(begin, end, step, 0)

    loop(1, exp_count, lambda k: spread(k).start())
    own.wait()
    for copy in weights:
        copy.start()
    loop(0, together + 2, gather_step)
    for copy in weights:
        copy.wait()
    tiles, wide_tiles = hid_ref.shape[1] // tile, width // wide_tile
    stride, wide_stride = max(1, tiles // together), max(1, wide_tiles // together)

    def group(p):
        base = p * together
        for i in range(together):
            complete(base + i)
            x_ref[pl.ds(i * chunk_rows, chunk_rows)] = buf[:, :, chunk(base + i)].reshape(chunk_rows, width)

        def hidden_tile(n):
            where = pl.ds(pl.multiple_of(n * tile, tile), tile)
            x = x_ref[...]
            gate = jnp.dot(x, gate_ref[:, where], preferred_element_type=jnp.float32)
            up = jnp.dot(x, up_ref[:, where], preferred_element_type=jnp.float32)
            hid_ref[:, where] = (jax.nn.silu(gate) * up).astype(hid_ref.dtype)

            @pl.when(lax.rem(n, stride) == 0)
            def _():
                gather_step(base + together + 2 + lax.div(n, stride))

        loop(0, tiles, hidden_tile)
        for i in range(together):
            for copy in directs(base + i) + relays(base + i):
                copy.wait_send()

        def down_tile(n):
            where = pl.ds(pl.multiple_of(n * wide_tile, wide_tile), wide_tile)
            y = jnp.dot(hid_ref[...], down_ref[:, where], preferred_element_type=jnp.float32).astype(buf.dtype)
            for i in range(together):
                buf[:, :, chunk(base + i), :, where] = y[i * chunk_rows : (i + 1) * chunk_rows].reshape(
                    OUTER, inner_count, capacity, wide_tile
                )

            @pl.when(lax.rem(n, wide_stride) == 0)
            def _():
                sum_step(base - 2 * together + lax.div(n, wide_stride))

        loop(0, wide_tiles, down_tile)
        for i in range(together):
            for copy in first(base + i):
                copy.start()

    loop(0, groups, group)
    loop(max(0, groups - 2) * together, exp_count + 1, sum_step)

    def finish(k):
        for copy in first(k) + second(k):
            copy.wait_send()

        @pl.when(k > 0)
        def _():
            spread(k).wait_send()
            third(k).wait_send()
            arrived(got_ref.at[lax.rem(e + k, exp_count)], g_send.at[k], g_recv.at[k])

    loop(0, exp_count, finish)
    stay().wait()


def experts(outgoing, w_gate, w_up, w_down, seq_count, exp_count):
    exp_count, capacity, width = outgoing.shape
    hidden = w_gate.shape[2]
    inner_count = seq_count // OUTER
    inner_peers = inner_count - 1
    half = width // 2
    kind = outgoing.dtype
    together = 1
    while 2 * together * seq_count * capacity <= 256 and exp_count % (2 * together) == 0:
        together *= 2
    rows = together * seq_count * capacity
    tile, wide_tile = min(256, hidden // together), min(512, width // together)
    vmem = [
        w_gate.shape[1:],
        w_up.shape[1:],
        w_down.shape[1:],
        (OUTER, inner_count, exp_count, capacity, width),
        (rows, width),
        (rows, hidden),
        (inner_peers, exp_count, OUTER, capacity, half),
        (exp_count, inner_count, capacity, half),
        (exp_count, capacity, half),
        (inner_peers, exp_count, capacity, half),
        (exp_count, capacity, half),
        (inner_peers, exp_count, capacity, half),
        (exp_count, capacity, width),
    ]
    one, per_peer, per_side = (exp_count,), (inner_count, exp_count), (2, inner_peers, exp_count)
    sems = [one, one, per_peer, per_peer, per_side, per_side, per_peer, per_peer, per_peer, per_peer, one, one]
    return pl.pallas_call(
        functools.partial(experts_kernel, seq_count, exp_count, together, tile, wide_tile),
        out_shape=jax.ShapeDtypeStruct((exp_count, capacity, width), kind),
        in_specs=[ANY] * 4,
        out_specs=ANY,
        scratch_shapes=[pltpu.VMEM(shape, kind) for shape in vmem]
        + [DMA, DMA((3,))]
        + [DMA(shape) for shape in sems],
        compiler_params=params(3, 60 * 1024 * 1024),
        name="experts",
    )(outgoing, w_gate, w_up, w_down)


def per_device(
    inputs, queries, keys, values, norm_gain, expert_ids, gate_weights, pairs, w_gate, w_up, w_down
):
    rows_dev, model_width = inputs.shape
    seq_count, exp_count = lax.axis_size("seq"), lax.axis_size("exp")
    query_run, keys_ext, values_ext = exchange_qkv(
        queries, keys, values, seq_count, exp_count, DIST * BLK
    )
    blocks_dev = query_run.shape[0] // BLK
    query_block = lax.axis_index("seq") * blocks_dev + jnp.arange(blocks_dev, dtype=jnp.int32)
    key_block = query_block[:, None] - (DIST - jnp.arange(DIST + 1, dtype=jnp.int32))[None, :]
    present = jnp.any(
        (pairs[None, None, :, 0] == query_block[:, None, None])
        & (pairs[None, None, :, 1] == key_block[:, :, None]),
        axis=2,
    ).astype(jnp.int32)
    attended = exchange_back(attend(query_run, keys_ext, values_ext, present), exp_count)
    mixed_sum = inputs.astype(jnp.float32) + attended.astype(jnp.float32)
    mean_square = jnp.mean(mixed_sum * mixed_sum, axis=1, keepdims=True)
    normed = (mixed_sum * lax.rsqrt(mean_square + norm_epsilon) * norm_gain[None, :]).astype(
        jnp.bfloat16
    )
    capacity = rows_dev * TOP // exp_count
    places = exp_count * capacity
    flat_ids = expert_ids.reshape(-1)
    id_table = (flat_ids[:, None] == jnp.arange(exp_count, dtype=jnp.int32)[None, :]).astype(
        jnp.int32
    )
    ahead_count = jnp.cumsum(id_table, axis=0) - id_table
    position = jnp.sum(ahead_count * id_table, axis=1)
    target = (flat_ids * capacity + position).reshape(rows_dev, TOP)
    slots = jnp.arange(places, dtype=jnp.int32)
    spots = target[:, :, None] == slots[None, None, :]
    choose = jnp.any(spots, axis=1).astype(jnp.bfloat16)
    outgoing = (
        lax.dot_general(choose, normed, (((0,), (0,)), ((), ())), preferred_element_type=jnp.float32)
        .astype(jnp.bfloat16)
        .reshape(exp_count, capacity, model_width)
    )
    got = experts(outgoing, w_gate, w_up, w_down, seq_count, exp_count)
    weight = jnp.sum(jnp.where(spots, gate_weights[:, :, None], 0.0), axis=1)
    coarse = weight.astype(jnp.bfloat16)
    fine = (weight - coarse.astype(jnp.float32)).astype(jnp.bfloat16)
    flat = got.reshape(places, model_width)
    combined = jnp.dot(coarse, flat, preferred_element_type=jnp.float32) + jnp.dot(
        fine, flat, preferred_element_type=jnp.float32
    )
    return (mixed_sum + combined).astype(jnp.bfloat16)


def solution(mesh):
    rows = P(("seq", "exp"), None)
    in_specs = (
        rows, rows, rows, rows, P(), rows, rows, P(),
        P("exp", None, "seq"), P("exp", None, "seq"), P("exp", "seq", None),
    )
    return jax.shard_map(
        per_device, mesh=mesh, in_specs=in_specs, out_specs=rows, check_vma=False
    )
```

```python
import functools
import math

import jax
import jax.numpy as jnp
from jax import lax
from jax.experimental import pallas as pl
from jax.experimental.pallas import tpu as pltpu
from jax.sharding import PartitionSpec as P

HSZ = 128
TOP = 2
BLK = 512
DIST = 2
OUTER = 2

very_negative = -1e30
norm_epsilon = 1e-05

MESH = pl.DeviceIdType.MESH
ANY = pl.BlockSpec(memory_space=pl.ANY)
DMA = pltpu.SemaphoreType.DMA


def remote(source, target, send_sem, recv_sem, device):
    return pltpu.make_async_remote_copy(
        src_ref=source,
        dst_ref=target,
        send_sem=send_sem,
        recv_sem=recv_sem,
        device_id=device,
        device_id_type=MESH,
    )


def enter(peers):
    barrier = pltpu.get_barrier_semaphore()
    for peer in peers:
        pl.semaphore_signal(barrier, inc=1, device_id=peer, device_id_type=MESH)
    pl.semaphore_wait(barrier, len(peers))


def turned(index, steps, count):
    return lax.rem(index + (steps % count), count)


def params(collective_id, vmem=None):
    return pltpu.CompilerParams(
        collective_id=collective_id, has_side_effects=True, vmem_limit_bytes=vmem
    )


def qkv_kernel(
    seq_count, exp_count, tail, q_ref, k_ref, v_ref, qr_ref, kx_ref, vx_ref,
    local_sem, z_send, z_recv, f_send, f_recv,
):
    s, e = lax.axis_index("seq"), lax.axis_index("exp")
    rows = q_ref.shape[0]
    group = qr_ref.shape[1]
    run = qr_ref.shape[0]
    arrays = ((k_ref, kx_ref, tail), (v_ref, vx_ref, tail), (q_ref, qr_ref, 0))
    enter(
        [(s, turned(e, k, exp_count)) for k in range(1, exp_count)]
        + [(turned(s, 1, seq_count), e), (turned(s, -1, seq_count), e)]
    )

    def columns(ref, index):
        return ref.at[:, pl.ds(pl.multiple_of(index * group, group), group)]

    def lines(ref, offset, index):
        return ref.at[pl.ds(pl.multiple_of(offset + index * rows, rows), rows)]

    waits = []
    for i, (source, target, offset) in enumerate(arrays):
        for k in range(1, exp_count):
            d = turned(e, k, exp_count)
            copy = remote(
                columns(source, d), lines(target, offset, e), z_send.at[i, k], z_recv.at[i, k], (s, d)
            )
            copy.start()
            waits.append(copy)
    locals_ = []
    for i, (source, target, offset) in enumerate(arrays):
        copy = pltpu.make_async_copy(columns(source, e), lines(target, offset, e), local_sem.at[i])
        copy.start()
        locals_.append(copy)

    def relay(i, k, act):
        source, target, offset = arrays[i]
        c = turned(e, -k, exp_count)
        inside = (c + 1) * rows > run - tail
        block = columns(source, e) if k == 0 else lines(target, offset, c)
        row = pl.multiple_of(lax.max(c * rows - (run - tail), 0), rows)
        copy = remote(
            block, target.at[pl.ds(row, rows)], f_send.at[i, k], f_recv.at[i, k],
            (turned(s, 1, seq_count), e),
        )
        if act == "start":
            pl.when(inside & (s < seq_count - 1))(copy.start)
        elif act == "send":
            pl.when(inside & (s < seq_count - 1))(copy.wait_send)
        else:
            pl.when(inside & (s > 0))(copy.wait_recv)

    for i in range(3):
        for k in range(exp_count):
            if k > 0:
                source, target, offset = arrays[i]
                block = lines(target, offset, turned(e, -k, exp_count))
                remote(block, block, z_send.at[i, k], z_recv.at[i, k], (s, e)).wait_recv()
            if i < 2:
                relay(i, k, "start")
    for i in range(2):
        for k in range(exp_count):
            relay(i, k, "recv")
            relay(i, k, "send")
    for copy in waits:
        copy.wait_send()
    for copy in locals_:
        copy.wait()


def exchange_qkv(queries, keys, values, seq_count, exp_count, tail):
    rows, width = queries.shape
    group, run = width // exp_count, rows * exp_count
    kind = queries.dtype
    return pl.pallas_call(
        functools.partial(qkv_kernel, seq_count, exp_count, tail),
        out_shape=(
            jax.ShapeDtypeStruct((run, group), kind),
            jax.ShapeDtypeStruct((tail + run, group), kind),
            jax.ShapeDtypeStruct((tail + run, group), kind),
        ),
        in_specs=[ANY] * 3,
        out_specs=(ANY,) * 3,
        scratch_shapes=[
            DMA((3,)),
            DMA((3, exp_count)),
            DMA((3, exp_count)),
            DMA((2, exp_count)),
            DMA((2, exp_count)),
        ],
        compiler_params=params(1),
        name="qkv_exchange",
    )(queries, keys, values)


def attend_kernel(
    seq_count, exp_count, slots, present_ref, q_ref, k_ref, v_ref, o_ref, att_ref, local_sem, z_send, z_recv
):
    s, e = lax.axis_index("seq"), lax.axis_index("exp")
    rows = o_ref.shape[0]
    run, group = q_ref.shape
    heads, blocks, owners = group // HSZ, run // BLK, BLK // rows
    scale = 1.0 / math.sqrt(HSZ)
    enter([(s, turned(e, k, exp_count)) for k in range(1, exp_count)])

    def source(owner, head):
        return att_ref.at[
            pl.ds(pl.multiple_of(owner * rows, rows), rows), pl.ds(pl.multiple_of(head * HSZ, HSZ), HSZ)
        ]

    def target(giver, head):
        return o_ref.at[:, pl.ds(pl.multiple_of(giver * group + head * HSZ, HSZ), HSZ)]

    def send(owner, head):
        return remote(
            source(owner, head), target(e, head), z_send.at[owner, head], z_recv.at[e, head], (s, owner)
        )

    def own(head):
        return pltpu.make_async_copy(source(e, head), target(e, head), local_sem.at[head])

    def step(i, carry):
        head = lax.rem(i, heads)
        block = lax.rem(lax.div(e, owners) + 1 + lax.div(i, heads), blocks)
        column = pl.ds(pl.multiple_of(head * HSZ, HSZ), HSZ)

        def lines(slot):
            return pl.ds(pl.multiple_of((block + slot) * BLK, BLK), BLK)

        q = q_ref[lines(0), column]
        scores = []
        for j in range(slots):
            score = lax.dot_general(
                q, k_ref[lines(j), column], (((1,), (1,)), ((), ())), preferred_element_type=jnp.float32
            )
            scores.append(jnp.where(present_ref[block, j] > 0, score * scale, very_negative))
        top = functools.reduce(jnp.maximum, [jnp.max(x, axis=1, keepdims=True) for x in scores])
        total, summed = 0.0, 0.0
        for j in range(slots):
            exps = jnp.exp(scores[j] - top)
            total = total + jnp.sum(exps, axis=1, keepdims=True)
            value = v_ref[lines(j), column]
            value = jnp.where(present_ref[block, j] > 0, value, jnp.zeros_like(value))
            summed = summed + jnp.dot(
                exps.astype(jnp.bfloat16), value, preferred_element_type=jnp.float32
            )
        att_ref[lines(0), column] = (summed / total).astype(att_ref.dtype)
        for j in range(owners):
            owner = block * owners + j

            @pl.when(owner != e)
            def _():
                send(owner, head).start()

            @pl.when(owner == e)
            def _():
                own(head).start()

        return carry

    lax.fori_loop(0, blocks * heads, step, 0)
    for head in range(heads):
        for k in range(1, exp_count):
            giver, owner = turned(e, -k, exp_count), turned(e, k, exp_count)
            block = target(giver, head)
            remote(block, block, z_send.at[giver, head], z_recv.at[giver, head], (s, e)).wait_recv()
            send(owner, head).wait_send()
        own(head).wait()


def attend(query_run, keys_ext, values_ext, present, seq_count, exp_count):
    run, group = query_run.shape
    heads = group // HSZ
    held = pl.BlockSpec(memory_space=pltpu.VMEM)
    return pl.pallas_call(
        functools.partial(attend_kernel, seq_count, exp_count, present.shape[1]),
        out_shape=jax.ShapeDtypeStruct((run // exp_count, group * exp_count), query_run.dtype),
        in_specs=[pl.BlockSpec(memory_space=pltpu.SMEM)] + [held] * 3,
        out_specs=ANY,
        scratch_shapes=[
            pltpu.VMEM((run, group), query_run.dtype),
            DMA((heads,)),
            DMA((exp_count, heads)),
            DMA((exp_count, heads)),
        ],
        compiler_params=params(2, 48 * 1024 * 1024),
        name="attend",
    )(present, query_run, keys_ext, values_ext)


def experts_kernel(
    seq_count, exp_count, together, tile, wide_tile,
    out_ref, gate_hbm, up_hbm, down_hbm, got_ref,
    gate_ref, up_ref, down_ref, buf, x_ref, hid_ref, in0, in1, out0, out1, mid0, mid1, done,
    local_sem, w_sem, z_send, z_recv, x_send, x_recv, d_send, d_recv,
    p_send, p_recv, m_send, m_recv, g_send, g_recv,
):
    s, e = lax.axis_index("seq"), lax.axis_index("exp")
    inner_count = seq_count // OUTER
    capacity, width = out_ref.shape[1:]
    half = width // 2
    a, b = lax.div(s, inner_count), lax.rem(s, inner_count)
    other = 1 - a
    outer = (other * inner_count + b, e)
    steps = range(1, inner_count)
    forth = [turned(b, j, inner_count) for j in steps]
    back = [turned(b, -j, inner_count) for j in steps]
    inner = [(a * inner_count + f, e) for f in forth]
    low, high = pl.ds(0, half), pl.ds(half, half)
    groups = exp_count // together
    chunk_rows = seq_count * capacity

    def chunk(k):
        return lax.rem(e - k + exp_count, exp_count)

    def arrived(block, send_sem, recv_sem):
        remote(block, block, send_sem, recv_sem, (s, e)).wait_recv()

    weights = [
        pltpu.make_async_copy(source.at[0], target, w_sem.at[i])
        for i, (source, target) in enumerate(
            ((gate_hbm, gate_ref), (up_hbm, up_ref), (down_hbm, down_ref))
        )
    ]
    own = pltpu.make_async_copy(out_ref.at[e], buf.at[a, b, e], local_sem)
    own.start()
    enter([(s, turned(e, k, exp_count)) for k in range(1, exp_count)] + [outer] + inner)

    def spread(k):
        d = lax.rem(e + k, exp_count)
        return remote(out_ref.at[d], buf.at[a, b, e], z_send.at[k], z_recv.at[k], (s, d))

    def directs(k):
        block = buf.at[a, b, chunk(k)]
        return [
            remote(block, block, x_send.at[i, k], x_recv.at[i, k], peer)
            for i, peer in enumerate([outer] + inner)
        ]

    def relays(k):
        c = chunk(k)
        copies = []
        for j, peer in enumerate(inner):
            block = buf.at[other, b, c, :, low]
            copies.append(remote(block, block, d_send.at[0, j, k], d_recv.at[0, j, k], peer))
            block = buf.at[a, back[j], c, :, high]
            copies.append(remote(block, block, d_send.at[1, j, k], d_recv.at[1, j, k], outer))
        return copies

    def gather_step(k):
        @pl.when(k < exp_count)
        def _():
            @pl.when(k > 0)
            def _():
                arrived(buf.at[a, b, chunk(k)], z_send.at[k], z_recv.at[k])

            for copy in directs(k):
                copy.start()

        @pl.when((k > 0) & (k <= exp_count))
        def _():
            n = k - 1
            c = chunk(n)
            arrived(buf.at[other, b, c], x_send.at[0, n], x_recv.at[0, n])
            for j in range(inner_count - 1):
                arrived(buf.at[a, back[j], c], x_send.at[1 + j, n], x_recv.at[1 + j, n])
            for copy in relays(n):
                copy.start()

    def complete(k):
        c = chunk(k)
        for j in range(inner_count - 1):
            for h, part in enumerate((low, high)):
                arrived(buf.at[other, back[j], c, :, part], d_send.at[h, j, k], d_recv.at[h, j, k])

    def first(k):
        c = chunk(k)
        return [
            remote(buf.at[other, :, c, :, high], in1.at[k], p_send.at[0, k], p_recv.at[0, k], outer)
        ] + [
            remote(
                buf.at[:, f, c, :, low], in0.at[j, k], p_send.at[1 + j, k], p_recv.at[1 + j, k], inner[j]
            )
            for j, f in enumerate(forth)
        ]

    def second(k):
        return [remote(out0.at[k], mid0.at[k], m_send.at[0, k], m_recv.at[0, k], outer)] + [
            remote(out1.at[j, k], mid1.at[j, k], m_send.at[1 + j, k], m_recv.at[1 + j, k], inner[j])
            for j in range(inner_count - 1)
        ]

    def third(k):
        return remote(done.at[k], got_ref.at[e], g_send.at[k], g_recv.at[k], (s, chunk(k)))

    def stay():
        return pltpu.make_async_copy(done.at[0], got_ref.at[e], local_sem)

    def wide(value):
        return value.astype(jnp.float32)

    def inner_sum(k, side):
        total = wide(buf[side, b, chunk(k), :, low])
        for j in range(inner_count - 1):
            total = total + wide(in0[j, k, side])
        return total

    def outer_sum(k, lane):
        return wide(buf[a, lane, chunk(k), :, high]) + wide(in1[k, lane])

    def sum_step(k):
        @pl.when((k >= 0) & (k < exp_count))
        def _():
            sends = second(k)
            for j in range(inner_count - 1):
                arrived(in0.at[j, k], p_send.at[1 + j, k], p_recv.at[1 + j, k])
            out0[k] = inner_sum(k, other).astype(out0.dtype)
            sends[0].start()
            arrived(in1.at[k], p_send.at[0, k], p_recv.at[0, k])
            for j, f in enumerate(forth):
                out1[j, k] = outer_sum(k, f).astype(out1.dtype)
                sends[1 + j].start()

        @pl.when((k > 0) & (k <= exp_count))
        def _():
            n = k - 1
            arrived(mid0.at[n], m_send.at[0, n], m_recv.at[0, n])
            done[n, :, low] = (inner_sum(n, a) + wide(mid0[n])).astype(done.dtype)
            total = outer_sum(n, b)
            for j in range(inner_count - 1):
                arrived(mid1.at[j, n], m_send.at[1 + j, n], m_recv.at[1 + j, n])
                total = total + wide(mid1[j, n])
            done[n, :, high] = total.astype(done.dtype)

            @pl.when(n == 0)
            def _():
                stay().start()

            @pl.when(n > 0)
            def _():
                third(n).start()

    def loop(begin, end, body):
        def step(i, carry):
            body(i)
            return carry

        lax.fori_loop(begin, end, step, 0)

    loop(1, exp_count, lambda k: spread(k).start())
    own.wait()
    for copy in weights:
        copy.start()
    loop(0, together + 2, gather_step)
    for copy in weights:
        copy.wait()
    tiles, wide_tiles = hid_ref.shape[1] // tile, width // wide_tile
    stride, wide_stride = max(1, tiles // together), max(1, wide_tiles // together)

    def group(p):
        base = p * together
        for i in range(together):
            complete(base + i)
            x_ref[pl.ds(i * chunk_rows, chunk_rows)] = buf[:, :, chunk(base + i)].reshape(chunk_rows, width)

        def hidden_tile(n):
            where = pl.ds(pl.multiple_of(n * tile, tile), tile)
            x = x_ref[...]
            gate = jnp.dot(x, gate_ref[:, where], preferred_element_type=jnp.float32)
            up = jnp.dot(x, up_ref[:, where], preferred_element_type=jnp.float32)
            hid_ref[:, where] = (jax.nn.silu(gate) * up).astype(hid_ref.dtype)

            @pl.when(lax.rem(n, stride) == 0)
            def _():
                gather_step(base + together + 2 + lax.div(n, stride))

        loop(0, tiles, hidden_tile)
        for i in range(together):
            for copy in directs(base + i) + relays(base + i):
                copy.wait_send()

        def down_tile(n):
            where = pl.ds(pl.multiple_of(n * wide_tile, wide_tile), wide_tile)
            y = jnp.dot(hid_ref[...], down_ref[:, where], preferred_element_type=jnp.float32).astype(buf.dtype)
            for i in range(together):
                buf[:, :, chunk(base + i), :, where] = y[i * chunk_rows : (i + 1) * chunk_rows].reshape(
                    OUTER, inner_count, capacity, wide_tile
                )

            @pl.when(lax.rem(n, wide_stride) == 0)
            def _():
                sum_step(base - together + lax.div(n, wide_stride))

        loop(0, wide_tiles, down_tile)
        for i in range(together):
            for copy in first(base + i):
                copy.start()

    loop(0, groups, group)
    loop((groups - 1) * together, exp_count + 1, sum_step)

    def finish(k):
        for copy in first(k) + second(k):
            copy.wait_send()

        @pl.when(k > 0)
        def _():
            spread(k).wait_send()
            third(k).wait_send()
            arrived(got_ref.at[lax.rem(e + k, exp_count)], g_send.at[k], g_recv.at[k])

    loop(0, exp_count, finish)
    stay().wait()


def experts(outgoing, w_gate, w_up, w_down, seq_count, exp_count):
    exp_count, capacity, width = outgoing.shape
    hidden = w_gate.shape[2]
    inner_count = seq_count // OUTER
    inner_peers = inner_count - 1
    half = width // 2
    kind = outgoing.dtype
    together = 1
    while 2 * together * seq_count * capacity <= 256 and exp_count % (2 * together) == 0:
        together *= 2
    rows = together * seq_count * capacity
    tile, wide_tile = min(256, hidden // together), min(512, width // together)
    vmem = [
        w_gate.shape[1:],
        w_up.shape[1:],
        w_down.shape[1:],
        (OUTER, inner_count, exp_count, capacity, width),
        (rows, width),
        (rows, hidden),
        (inner_peers, exp_count, OUTER, capacity, half),
        (exp_count, inner_count, capacity, half),
        (exp_count, capacity, half),
        (inner_peers, exp_count, capacity, half),
        (exp_count, capacity, half),
        (inner_peers, exp_count, capacity, half),
        (exp_count, capacity, width),
    ]
    one, per_peer, per_side = (exp_count,), (inner_count, exp_count), (2, inner_peers, exp_count)
    sems = [one, one, per_peer, per_peer, per_side, per_side, per_peer, per_peer, per_peer, per_peer, one, one]
    return pl.pallas_call(
        functools.partial(experts_kernel, seq_count, exp_count, together, tile, wide_tile),
        out_shape=jax.ShapeDtypeStruct((exp_count, capacity, width), kind),
        in_specs=[ANY] * 4,
        out_specs=ANY,
        scratch_shapes=[pltpu.VMEM(shape, kind) for shape in vmem]
        + [DMA, DMA((3,))]
        + [DMA(shape) for shape in sems],
        compiler_params=params(3, 60 * 1024 * 1024),
        name="experts",
    )(outgoing, w_gate, w_up, w_down)


def per_device(
    inputs, queries, keys, values, norm_gain, expert_ids, gate_weights, pairs, w_gate, w_up, w_down
):
    rows_dev, model_width = inputs.shape
    seq_count, exp_count = lax.axis_size("seq"), lax.axis_size("exp")
    query_run, keys_ext, values_ext = exchange_qkv(
        queries, keys, values, seq_count, exp_count, DIST * BLK
    )
    blocks_dev = query_run.shape[0] // BLK
    query_block = lax.axis_index("seq") * blocks_dev + jnp.arange(blocks_dev, dtype=jnp.int32)
    key_block = query_block[:, None] - (DIST - jnp.arange(DIST + 1, dtype=jnp.int32))[None, :]
    present = jnp.any(
        (pairs[None, None, :, 0] == query_block[:, None, None])
        & (pairs[None, None, :, 1] == key_block[:, :, None]),
        axis=2,
    ).astype(jnp.int32)
    attended = attend(query_run, keys_ext, values_ext, present, seq_count, exp_count)
    mixed_sum = inputs.astype(jnp.float32) + attended.astype(jnp.float32)
    mean_square = jnp.mean(mixed_sum * mixed_sum, axis=1, keepdims=True)
    normed = (mixed_sum * lax.rsqrt(mean_square + norm_epsilon) * norm_gain[None, :]).astype(
        jnp.bfloat16
    )
    capacity = rows_dev * TOP // exp_count
    places = exp_count * capacity
    flat_ids = expert_ids.reshape(-1)
    id_table = (flat_ids[:, None] == jnp.arange(exp_count, dtype=jnp.int32)[None, :]).astype(
        jnp.int32
    )
    ahead_count = jnp.cumsum(id_table, axis=0) - id_table
    position = jnp.sum(ahead_count * id_table, axis=1)
    target = (flat_ids * capacity + position).reshape(rows_dev, TOP)
    slots = jnp.arange(places, dtype=jnp.int32)
    spots = target[:, :, None] == slots[None, None, :]
    choose = jnp.any(spots, axis=1).astype(jnp.bfloat16)
    outgoing = (
        lax.dot_general(choose, normed, (((0,), (0,)), ((), ())), preferred_element_type=jnp.float32)
        .astype(jnp.bfloat16)
        .reshape(exp_count, capacity, model_width)
    )
    got = experts(outgoing, w_gate, w_up, w_down, seq_count, exp_count)
    weight = jnp.sum(jnp.where(spots, gate_weights[:, :, None], 0.0), axis=1)
    coarse = weight.astype(jnp.bfloat16)
    fine = (weight - coarse.astype(jnp.float32)).astype(jnp.bfloat16)
    flat = got.reshape(places, model_width)
    combined = jnp.dot(coarse, flat, preferred_element_type=jnp.float32) + jnp.dot(
        fine, flat, preferred_element_type=jnp.float32
    )
    return (mixed_sum + combined).astype(jnp.bfloat16)


def solution(mesh):
    rows = P(("seq", "exp"), None)
    in_specs = (
        rows, rows, rows, rows, P(), rows, rows, P(),
        P("exp", None, "seq"), P("exp", None, "seq"), P("exp", "seq", None),
    )
    return jax.shard_map(
        per_device, mesh=mesh, in_specs=in_specs, out_specs=rows, check_vma=False
    )
```
